32 devices in a mesh: vocab: 8 (over z, y), feat: 4 (over x, core).
Axes of the slice: x: 2, y: 2, z: 4, core: 2. Of those that a mesh axis runs over, the one named last changes fastest.
Arguments:
- hidden: bfloat16 [1024, 4096], P('feat'), may hold values from -64 to 64
- out_head: bfloat16 [32768, 4096], P(('vocab', 'feat')), may hold values from -0.28125 to 0.28125
- out_proj: bfloat16 [32768, 128], P(('vocab', 'feat')), may hold values from -5 to 5
- in_proj: bfloat16 [4096, 128], replicated, may hold values from -0.09375 to 0.09375
- targets: int32 [1024], replicated, may hold values from 0 to 32767
- seq_ids: int32 [1024], replicated, may hold values from 0 to 15, never falling along the last dimension, each value on 1 to 128 neighbouring positions
- grad_store: bfloat16 [16384, 16384], P('vocab', 'feat'), may hold values from -0.01953125 to 0.01953125
Outputs:
- influence: float32 [16384, 16], P(('vocab', 'feat'))
The draws below stay inside these ranges and needn't reach their ends.
All inputs are finite; a program needn't handle non-finite values.
Results may differ from the reference program's by a relative error of at most 0.003.
Values may be sent and summed in bfloat16 or wider, within the bound.
A program may use at most 128 MiB of HBM per device.

```python
import math
import jax
import jax.numpy as jnp
import numpy as np
from jax import lax

D = 4096
R = 128
SEQS = 16
VOCAB = 32768
TOKENS = 1024
EXAMPLES = 16384
FEATS = 16384


def head_rows(key, row_ids):
    base_key = jax.random.fold_in(key, 7)

    def single(row_id):
        values = jax.random.normal(jax.random.fold_in(base_key, row_id), (D,), jnp.float32)
        return jnp.clip(values, -6.0, 6.0) * (3.0 / math.sqrt(D))
    return jax.vmap(single)(row_ids)


def draw_out_head(key, part):
    return head_rows(key, jnp.arange(VOCAB, dtype=jnp.int32)).astype(jnp.bfloat16)


def draw_hidden(key, part):
    values = jnp.clip(jax.random.normal(jax.random.fold_in(key, 3), (TOKENS, D), jnp.float32), -5.0, 5.0)
    return values.astype(jnp.bfloat16)


def place_ends(drawn, rng, low, high):
    longest = drawn.shape.index(max(drawn.shape))
    spots = []
    for shift in (0, 1):
        where = [jax.random.randint(jax.random.fold_in(rng, axis), (), 0, length) for axis, length in enumerate(drawn.shape)]
        where[longest] = (where[longest] + shift) % drawn.shape[longest]
        spots.append(tuple(where))
    return drawn.at[spots[0]].set(low).at[spots[1]].set(high)


def with_spikes(result, stream_key, source, target, blocks, factor):
    owner, partner = [(jnp.arange(result.shape[position]) // (result.shape[position] // blocks)).reshape([-1 if axis == position else 1 for axis in range(result.ndim)]) for position in (source, target)]
    chosen = jax.random.permutation(stream_key, blocks)[partner]
    strong = (owner == chosen) | (owner == (partner + blocks // 2) % blocks)
    return jnp.where(strong, factor * result, result)


def block_scale(own_key, shape, split, smallest, top_value):
    def one(position, parts):
        draws = jax.random.uniform(jax.random.fold_in(jax.random.fold_in(own_key, 6), position), (parts,), jnp.float32, smallest / len(split), top_value / len(split))
        return jnp.repeat(jnp.exp(draws), shape[position] // parts).reshape((-1,) + (1,) * (len(shape) - position - 1))

    level = one(*split[0])
    for cut in split[1:]:
        level = level * one(*cut)
    return level


def split_up(amount, total, most, lean):
    loads = [(1 << 20) // math.isqrt(standing ** lean) + 1 for standing in range(2, amount + 1)]
    spare, holding = total - most - (amount - 1), [1] * (amount - 1)
    while spare > 0:
        candidates = [i for i in range(amount - 1) if holding[i] < most]
        pool, remaining = sum([loads[i] for i in candidates]), spare
        for i in candidates:
            more = min(most - holding[i], max(1, remaining * loads[i] // pool), spare)
            holding[i] = holding[i] + more
            spare = spare - more
    return np.array([most] + holding)


def ragged_sizes(key, number_of, total, reach, lean):
    if number_of == 2:
        one = jax.random.randint(key, (), max(1, total - reach), min(reach, total - 1) + 1)
        return jnp.stack([one, total - one])
    sizes = jnp.asarray(split_up(number_of, total, reach, lean), jnp.int32)
    couples = (number_of - 1) // 2
    donor, sink = sizes[1:1 + 2 * couples:2], sizes[2:2 + 2 * couples:2]
    margin = jnp.minimum(donor - 1, reach - sink)
    moved = jax.random.randint(jax.random.fold_in(key, 1), (couples,), 0, 1 << 20) % (margin + 1)
    sizes = sizes.at[1:1 + 2 * couples:2].set(donor - moved).at[2:2 + 2 * couples:2].set(sink + moved)
    return sizes[jax.random.permutation(jax.random.fold_in(key, 2), number_of)]


def bell_draw(key, shape, scale, limit, cuts=(), kind=jnp.bfloat16):
    drawn = jax.random.normal(key, shape, jnp.float32) * scale
    if len(cuts) > 0:
        drawn = block_scale(key, shape, cuts, -0.22, 0.18) * drawn
    return jnp.clip(drawn, min=-limit, max=limit).astype(kind)


def gaussian_with(key, shape, width, bound, split, heavy, kind=jnp.bfloat16):
    entries = width * jax.random.normal(key, shape, jnp.float32)
    if split:
        entries = entries * block_scale(key, shape, split, -0.22, 0.18)
    return jnp.clip(with_spikes(entries, jax.random.fold_in(key, 3), *heavy), -bound, bound).astype(kind)


def setup_inputs(seed: int = 0) -> dict:
    keys = jax.random.split(jax.random.key(seed), 8)
    return {
        "hidden": draw_hidden(jax.random.fold_in(keys[7], 71), 0),
        "out_head": draw_out_head(jax.random.fold_in(keys[7], 71), 0),
        "out_proj": bell_draw(keys[2], (VOCAB, R), 1.0, 5.0, ((0, 32),)),
        "in_proj": bell_draw(keys[3], (D, R), D ** -0.5, 0.09375),
        "targets": place_ends(jax.random.randint(keys[4], (TOKENS,), 0, VOCAB), jax.random.fold_in(keys[4], 1), 0, VOCAB - 1).astype(jnp.int32),
        "seq_ids": jnp.searchsorted(jnp.cumsum(ragged_sizes(keys[5], SEQS, TOKENS, 2 * TOKENS // SEQS, 0)), jnp.arange(TOKENS), side="right").astype(jnp.int32),
        "grad_store": gaussian_with(keys[6], (EXAMPLES, FEATS), (1.0 / (8.0 * R)), 0.01953125, ((0, 8), (1, 4)), (1, 0, 8, 2.0)),
    }


def reference(hidden, out_head, out_proj, in_proj, targets, seq_ids, grad_store):
    logits = jnp.dot(hidden, out_head.T, preferred_element_type=jnp.float32)
    row_max = jnp.max(logits, axis=1, keepdims=True)
    expval = jnp.exp(logits - row_max)
    row_sum = jnp.sum(expval, axis=1, keepdims=True)
    columns = jnp.arange(VOCAB, dtype=jnp.int32)
    onehot = (targets[:, None] == columns[None, :]).astype(jnp.float32)
    residual = (expval / row_sum - onehot).astype(jnp.bfloat16)
    out_side = jnp.dot(residual, out_proj, preferred_element_type=jnp.float32)
    in_side = jnp.dot(hidden, in_proj, preferred_element_type=jnp.float32)
    member = (seq_ids[:, None] == jnp.arange(SEQS, dtype=jnp.int32)[None, :]).astype(jnp.float32)
    query_grads = jnp.einsum("ts,ti,tj->sij", member, out_side, in_side, precision=lax.Precision.HIGHEST)
    query_grads = query_grads.reshape(SEQS, R * R).astype(jnp.bfloat16)
    return jnp.dot(grad_store, query_grads.T, preferred_element_type=jnp.float32)
```

```python
import functools

import jax
import jax.numpy as jnp
from jax import lax
from jax.experimental import pallas as pl
from jax.experimental.pallas import tpu as pltpu
from jax.sharding import PartitionSpec as P

SEQS = 16
SUBS = 4
F32 = jnp.float32
BF16 = jnp.bfloat16
NT = (((1,), (1,)), ((), ()))


def kernel(nv, nf, hid_in, head_in, oproj, iproj_in, targets, seqs, gs_in, out,
           hid, head, iproj, gs, lg, o_t, o_full, ins, sv, so, st, rv, ro, rst, osb, qg, qgm, part, infl,
           load_sem, x_send, y_send, z_send, s_send, recv, s_recv, own_sems,
           sv_send, so_send, st_send, rv_sem, ro_sem, rst_sem, ag_send, ag_recv, in_send, in_recv, loc_sem):
    v = lax.axis_index("vocab")
    f = lax.axis_index("feat")
    me = v * nf + f
    nd = nv * nf
    x, k = f // 2, f % 2
    xn = nf // 2
    sib = f + 1 - 2 * k
    vy = v + 1 - 2 * (v % 2)
    vz = v + 2 - 4 * ((v // 2) % 2)
    tl = hid.shape[1]
    vl = head.shape[0]
    rank = oproj.shape[1]
    rf, tb = sv.shape[1], sv.shape[2]
    bpc = tl // tb
    eo = out.shape[1]
    piece = tl // 4
    sr = piece // SUBS

    loads = [
        pltpu.make_async_copy(hid_in, hid.at[f], load_sem.at[0]),
        pltpu.make_async_copy(head_in, head, load_sem.at[1]),
        pltpu.make_async_copy(iproj_in, iproj, load_sem.at[2]),
        pltpu.make_async_copy(gs_in, gs, load_sem.at[3]),
    ]
    loads[0].start()
    loads[1].start()
    loads[2].start()

    barrier = pltpu.get_barrier_semaphore()

    def greet(p, c):
        d = (me + p) % nd
        pl.semaphore_signal(barrier, inc=1, device_id={"vocab": d // nf, "feat": d % nf},
                            device_id_type=pl.DeviceIdType.MESH)
        return c

    lax.fori_loop(1, nd, greet, 0)
    pl.semaphore_wait(barrier, nd - 1)

    def remote(src, dst, ss, rs, dv, df):
        return pltpu.make_async_remote_copy(
            src_ref=src, dst_ref=dst, send_sem=ss, recv_sem=rs,
            device_id={"vocab": dv, "feat": df}, device_id_type=pl.DeviceIdType.MESH)

    def rows(fi, owner, j):
        return hid.at[fi, pl.ds(pl.multiple_of((owner % 4) * piece + j * sr, sr), sr)]

    pending = []

    def go(copy):
        copy.start()
        pending.append(copy)

    loads[0].wait()
    for r in range(xn - 1):
        fo = 2 * ((x + r + 1) % xn) + k
        for j in range(SUBS):
            go(remote(rows(f, v, j), rows(f, v, j), x_send.at[r, j], recv.at[r, 0, j], v, fo))
    own = remote(hid.at[f], hid.at[f], own_sems.at[0], own_sems.at[1], v, sib)
    go(own)
    loads[3].start()

    def src_of(r):
        return 2 * ((x + xn - r - 1) % xn) + k

    vd = vy + vz - v
    owners = (v, vy, vz, vd)

    def arrive(r, rel, j):
        fi = src_of(r)
        blk = rows(fi, owners[rel], j)
        remote(blk, blk, x_send.at[r, j], recv.at[r, rel, j], v, f).wait_recv()
        half = j < SUBS // 2
        if rel == 0:
            go(remote(blk, blk, y_send.at[r, 0, j], recv.at[r, 1, j], vy, f))
            go(remote(blk, blk, z_send.at[r, 0, j], recv.at[r, 2, j], vz, f))
        if rel == 1 and half:
            go(remote(blk, blk, z_send.at[r, 1, j], recv.at[r, 3, j], vz, f))
        if rel == 2 and not half:
            go(remote(blk, blk, y_send.at[r, 1, j], recv.at[r, 3, j], vy, f))
        go(remote(blk, blk, s_send.at[r, rel, j], s_recv.at[r, rel, j], v, sib))

    def post(send_buf, recv_buf, sends, recvs, d):
        @pl.when(d != me)
        def _():
            remote(send_buf, recv_buf, sends.at[d], recvs.at[me], d // nf, d % nf).start()

    o_t[...] = oproj[...].astype(F32).T.astype(BF16)
    base = me * vl

    def onehot_step(c, carry):
        ids = lax.broadcasted_iota(jnp.int32, (vl, tl), 0) + base
        hot = (targets[c] == ids).astype(F32).astype(BF16)
        o = jnp.dot(o_t[...], hot, preferred_element_type=F32)
        o_full[c] = o
        for b in range(bpc):
            for g in range(nf):
                d = (c * bpc + b) * nf + g
                so[d] = o[g * rf:(g + 1) * rf, b * tb:(b + 1) * tb].astype(BF16)
        for b in range(bpc):
            for g in range(nf):
                d = (c * bpc + b) * nf + g
                post(so.at[d], ro.at[me], so_send, ro_sem, d)
        return carry

    lax.fori_loop(0, nf, onehot_step, 0)

    vt = min(256, vl)
    nt = vl // vt

    def tiles(fi, lo, hi, m):
        def tile(i, m):
            at = pl.ds(pl.multiple_of(i * vt, vt), vt)
            l = lax.dot_general(head[at, :], hid[fi], NT, preferred_element_type=F32)
            lg[at, :] = l
            return jnp.maximum(m, jnp.max(l, axis=0, keepdims=True))
        return lax.fori_loop(lo, hi, tile, m)

    def finish(fi, m):
        e = jnp.exp(lg[...] - m)
        s = jnp.sum(e, axis=0, keepdims=True)
        u = jnp.dot(o_t[...], e.astype(BF16), preferred_element_type=F32)
        u = u / s - o_full[fi]
        for b in range(bpc):
            lanes = slice(b * tb, (b + 1) * tb)
            blk = fi * bpc + b
            st[blk, 0:1, :] = m[:, lanes]
            st[blk, 1:2, :] = s[:, lanes]
            for g in range(nf):
                sv[blk * nf + g] = u[g * rf:(g + 1) * rf, lanes].astype(BF16)
        for b in range(bpc):
            for g in range(nf):
                blk = fi * bpc + b
                d = blk * nf + g
                post(st.at[blk], rst.at[me], st_send, rst_sem, d)
                post(sv.at[d], rv.at[me], sv_send, rv_sem, d)
        ins[fi] = jnp.dot(hid[fi], iproj[...], preferred_element_type=F32)

    low = jnp.full((1, tl), -jnp.inf, F32)
    loads[1].wait()
    loads[2].wait()
    every = range(xn - 1)
    for r in every:
        arrive(r, 0, 0)
    m = tiles(f, 0, nt // 2, low)
    for r in every:
        arrive(r, 0, 1)
    m = tiles(f, nt // 2, nt, m)
    for r in every:
        arrive(r, 1, 0)
        arrive(r, 2, 0)
        arrive(r, 0, 2)
    finish(f, m)
    remote(hid.at[f], hid.at[sib], own_sems.at[0], own_sems.at[1], v, sib).wait_recv()
    m = tiles(sib, 0, nt // 2, low)
    for r in every:
        arrive(r, 1, 1)
        arrive(r, 2, 1)
        arrive(r, 0, 3)
    m = tiles(sib, nt // 2, nt, m)
    for r in every:
        arrive(r, 1, 2)
        arrive(r, 2, 2)
    finish(sib, m)
    for j in range(3, SUBS):
        for r in every:
            arrive(r, 1, j)
            arrive(r, 2, j)
    for j in range(SUBS):
        for r in every:
            arrive(r, 3, j)

    def remote_chunk(fi):
        finish(fi, tiles(fi, 0, nt, low))

    for r in every:
        remote_chunk(src_of(r))
    for r in every:
        fs = src_of(r) + 1 - 2 * k
        for rel in range(4):
            for j in range(SUBS):
                blk = rows(fs, owners[rel], j)
                remote(blk, blk, s_send.at[r, rel, j], s_recv.at[r, rel, j], v, sib).wait_recv()
        remote_chunk(fs)

    for a, b, i in ((sv, rv, 0), (so, ro, 1)):
        pltpu.make_async_copy(a.at[me], b.at[me], loc_sem.at[i]).start()
    pltpu.make_async_copy(st.at[v], rst.at[me], loc_sem.at[2]).start()
    for a, b, i in ((sv, rv, 0), (so, ro, 1)):
        pltpu.make_async_copy(a.at[me], b.at[me], loc_sem.at[i]).wait()
    pltpu.make_async_copy(st.at[v], rst.at[me], loc_sem.at[2]).wait()

    def take(p, c):
        d = (me + p) % nd
        remote(st.at[v], rst.at[d], st_send.at[d], rst_sem.at[d], v, f).wait_recv()
        remote(so.at[d], ro.at[d], so_send.at[d], ro_sem.at[d], v, f).wait_recv()
        remote(sv.at[d], rv.at[d], sv_send.at[d], rv_sem.at[d], v, f).wait_recv()
        return c

    lax.fori_loop(1, nd, take, 0)
    top = lax.fori_loop(0, nd, lambda d, t: jnp.maximum(t, rst[d, 0:1, :]), jnp.full((1, tb), -jnp.inf, F32))
    total = lax.fori_loop(
        0, nd, lambda d, t: t + jnp.exp(rst[d, 0:1, :] - top) * rst[d, 1:2, :], jnp.zeros((1, tb), F32))

    def add(d, acc):
        w = jnp.exp(rst[d, 0:1, :] - top) * rst[d, 1:2, :] / total
        return acc + w * rv[d].astype(F32) - (1.0 - w) * ro[d].astype(F32)

    osb[v] = lax.fori_loop(0, nd, add, jnp.zeros((rf, tb), F32))

    def spread(p, c):
        dv = (v + p) % nv
        remote(osb.at[v], osb.at[v], ag_send.at[p], ag_recv.at[v], dv, f).start()
        return c

    lax.fori_loop(1, nv, spread, 0)

    qg[...] = jnp.zeros_like(qg)

    def outer(p, c):
        b = (v + p) % nv

        @pl.when(p > 0)
        def _():
            remote(osb.at[b], osb.at[b], ag_send.at[p], ag_recv.at[b], v, f).wait_recv()

        member = (seqs[b] == lax.broadcasted_iota(jnp.int32, (SEQS, tb), 0)).astype(F32)
        o = osb[b]
        weighted = jnp.concatenate([member * o[i:i + 1, :] for i in range(rf)], axis=0)
        act = ins[b // bpc, pl.ds(pl.multiple_of((b % bpc) * tb, tb), tb), :]
        qg[...] += jnp.dot(weighted, act, preferred_element_type=F32, precision=lax.Precision.HIGHEST)
        return c

    lax.fori_loop(0, nv, outer, 0)
    for i in range(rf):
        qgm[:, i * rank:(i + 1) * rank] = qg[i * SEQS:(i + 1) * SEQS, :].astype(BF16)
    loads[3].wait()

    def score(p, c):
        g = (f + p) % nf
        part[g] = lax.dot_general(
            qgm[...], gs[pl.ds(pl.multiple_of(g * eo, eo), eo), :], NT, preferred_element_type=F32)

        @pl.when(p < nf)
        def _():
            remote(part.at[g], infl.at[f], in_send.at[p % nf], in_recv.at[f], v, g).start()
        return c

    lax.fori_loop(1, nf + 1, score, 0)
    result = part[f]
    for p in range(1, nf):
        g = (f + p) % nf
        remote(part.at[g], infl.at[g], in_send.at[p], in_recv.at[g], v, g).wait_recv()
        result = result + infl[g]
    out[...] = result

    for copy in pending:
        copy.wait_send()

    def drain(p, c):
        d = (me + p) % nd
        remote(st.at[d // nf], rst.at[me], st_send.at[d], rst_sem.at[me], v, f).wait_send()
        remote(so.at[d], ro.at[me], so_send.at[d], ro_sem.at[me], v, f).wait_send()
        remote(sv.at[d], rv.at[me], sv_send.at[d], rv_sem.at[me], v, f).wait_send()
        return c

    lax.fori_loop(1, nd, drain, 0)
    for p in range(1, nv):
        remote(osb.at[v], osb.at[v], ag_send.at[p], ag_recv.at[v], v, f).wait_send()
    for p in range(1, nf):
        g = (f + p) % nf
        remote(part.at[g], infl.at[f], in_send.at[p], in_recv.at[f], v, f).wait_send()


def solution(mesh):
    nv, nf = mesh.shape["vocab"], mesh.shape["feat"]
    nd = nv * nf
    xn = nf // 2

    def on_device(hidden, out_head, out_proj, in_proj, targets, seq_ids, grad_store):
        tl, width = hidden.shape
        vl, rank = out_proj.shape
        el, fl = grad_store.shape
        tokens = tl * nf
        rf, tb, eo = rank // nf, tokens // nv, el // nf
        any_spec = pl.BlockSpec(memory_space=pl.ANY)
        vmem = pl.BlockSpec(memory_space=pltpu.VMEM)
        dma = pltpu.SemaphoreType.DMA
        res = pl.pallas_call(
            functools.partial(kernel, nv, nf),
            out_shape=jax.ShapeDtypeStruct((SEQS, eo), F32),
            in_specs=[any_spec, any_spec, vmem, any_spec, vmem, vmem, any_spec],
            out_specs=vmem,
            scratch_shapes=[
                pltpu.VMEM((nf, tl, width), BF16),
                pltpu.VMEM((vl, width), BF16),
                pltpu.VMEM((width, rank), BF16),
                pltpu.VMEM((el, fl), BF16),
                pltpu.VMEM((vl, tl), F32),
                pltpu.VMEM((rank, vl), BF16),
                pltpu.VMEM((nf, rank, tl), F32),
                pltpu.VMEM((nf, tl, rank), F32),
                pltpu.VMEM((nd, rf, tb), BF16),
                pltpu.VMEM((nd, rf, tb), BF16),
                pltpu.VMEM((nv, 8, tb), F32),
                pltpu.VMEM((nd, rf, tb), BF16),
                pltpu.VMEM((nd, rf, tb), BF16),
                pltpu.VMEM((nd, 8, tb), F32),
                pltpu.VMEM((nv, rf, tb), F32),
                pltpu.VMEM((rf * SEQS, rank), F32),
                pltpu.VMEM((SEQS, fl), BF16),
                pltpu.VMEM((nf, SEQS, eo), F32),
                pltpu.VMEM((nf, SEQS, eo), F32),
                dma((4,)),
                dma((xn - 1, SUBS)),
                dma((xn - 1, 2, SUBS)),
                dma((xn - 1, 2, SUBS)),
                dma((xn - 1, 4, SUBS)),
                dma((xn - 1, 4, SUBS)),
                dma((xn - 1, 4, SUBS)),
                dma((2,)),
                dma((nd,)),
                dma((nd,)),
                dma((nd,)),
                dma((nd,)),
                dma((nd,)),
                dma((nd,)),
                dma((nv,)),
                dma((nv,)),
                dma((nf,)),
                dma((nf,)),
                dma((3,)),
            ],
            compiler_params=pltpu.CompilerParams(
                collective_id=0, has_side_effects=True, vmem_limit_bytes=60 * 1024 * 1024),
        )(hidden, out_head, out_proj, in_proj, targets.reshape(nf, 1, tl), seq_ids.reshape(nv, 1, tb), grad_store)
        return res.T

    in_specs = (
        P("feat", None),
        P(("vocab", "feat"), None),
        P(("vocab", "feat"), None),
        P(),
        P(),
        P(),
        P("vocab", "feat"),
    )
    return jax.shard_map(
        on_device, mesh=mesh, in_specs=in_specs, out_specs=P(("vocab", "feat"), None), check_vma=False
    )
```

```python
import functools

import jax
import jax.numpy as jnp
from jax import lax
from jax.experimental import pallas as pl
from jax.experimental.pallas import tpu as pltpu
from jax.sharding import PartitionSpec as P

SEQS = 16
SUBS = 4
F32 = jnp.float32
BF16 = jnp.bfloat16
NT = (((1,), (1,)), ((), ()))


def kernel(nv, nf, hid_in, head_in, oproj, iproj_in, targets, seqs, gs_in, out,
           hid, head, iproj, gs, lg, o_t, o_full, ins, sv, so, st, rv, ro, rst, osb, qg, qgm, part, infl,
           load_sem, x_send, y_send, z_send, s_send, recv, s_recv, own_sems,
           sv_send, so_send, st_send, rv_sem, ro_sem, rst_sem, ag_send, ag_recv, in_send, in_recv, loc_sem):
    v = lax.axis_index("vocab")
    f = lax.axis_index("feat")
    me = v * nf + f
    nd = nv * nf
    x, k = f // 2, f % 2
    xn = nf // 2
    sib = f + 1 - 2 * k
    vy = v + 1 - 2 * (v % 2)
    vz = v + 2 - 4 * ((v // 2) % 2)
    vl = head.shape[0]
    rank = oproj.shape[1]
    rf, tb = sv.shape[1], sv.shape[2]
    parts = hid.shape[1]
    tc = 2 * tb
    eo = out.shape[1]
    piece = tb // 4
    per = SUBS // parts
    sr = piece // per

    loads = [
        pltpu.make_async_copy(head_in, head, load_sem.at[0]),
        pltpu.make_async_copy(iproj_in, iproj, load_sem.at[1]),
        pltpu.make_async_copy(gs_in, gs, load_sem.at[2]),
    ]

    def half(xi, kk, h):
        return hid.at[xi, h, pl.ds(pl.multiple_of(kk * tb, tb), tb)]

    mine = [pltpu.make_async_copy(hid_in.at[pl.ds(h * tb, tb)], half(x, k, h), load_sem.at[3 + h])
            for h in range(parts)]
    for copy in mine + loads[:2]:
        copy.start()

    barrier = pltpu.get_barrier_semaphore()

    def greet(p, c):
        d = (me + p) % nd
        pl.semaphore_signal(barrier, inc=1, device_id={"vocab": d // nf, "feat": d % nf},
                            device_id_type=pl.DeviceIdType.MESH)
        return c

    lax.fori_loop(1, nd, greet, 0)
    pl.semaphore_wait(barrier, nd - 1)

    def remote(src, dst, ss, rs, dv, df):
        return pltpu.make_async_remote_copy(
            src_ref=src, dst_ref=dst, send_sem=ss, recv_sem=rs,
            device_id={"vocab": dv, "feat": df}, device_id_type=pl.DeviceIdType.MESH)

    def rows(xi, kk, owner, j):
        at = kk * tb + (owner % 4) * piece + (j % per) * sr
        return hid.at[xi, j // per, pl.ds(pl.multiple_of(at, sr), sr)]

    pending = []

    def go(copy):
        copy.start()
        pending.append(copy)

    for h in range(parts):
        mine[h].wait()
        for r in range(xn - 1):
            fo = 2 * ((x + r + 1) % xn) + k
            for j in range(h * per, (h + 1) * per):
                blk = rows(x, k, v, j)
                go(remote(blk, blk, x_send.at[r, j], recv.at[r, 0, j], v, fo))
        go(remote(half(x, k, h), half(x, k, h), own_sems.at[0, h], own_sems.at[1, h], v, sib))
    loads[2].start()

    def src_of(r):
        return (x + xn - r - 1) % xn

    vd = vy + vz - v
    owners = (v, vy, vz, vd)

    def arrive(r, rel, j):
        blk = rows(src_of(r), k, owners[rel], j)
        remote(blk, blk, x_send.at[r, j], recv.at[r, rel, j], v, f).wait_recv()
        first = j % per < per // 2
        if rel == 0:
            go(remote(blk, blk, y_send.at[r, 0, j], recv.at[r, 1, j], vy, f))
            go(remote(blk, blk, z_send.at[r, 0, j], recv.at[r, 2, j], vz, f))
        if rel == 1 and first:
            go(remote(blk, blk, z_send.at[r, 1, j], recv.at[r, 3, j], vz, f))
        if rel == 2 and not first:
            go(remote(blk, blk, y_send.at[r, 1, j], recv.at[r, 3, j], vy, f))
        go(remote(blk, blk, s_send.at[r, rel, j], s_recv.at[r, rel, j], v, sib))

    def post(send_buf, recv_buf, sends, recvs, d):
        @pl.when(d != me)
        def _():
            remote(send_buf, recv_buf, sends.at[d], recvs.at[me], d // nf, d % nf).start()

    o_t[...] = oproj[...].astype(F32).T.astype(BF16)
    base = me * vl

    def onehot_step(c, carry):
        xi, h = c // parts, c % parts
        blks = [(2 * xi + kk) * parts + h for kk in range(2)]
        ids = lax.broadcasted_iota(jnp.int32, (vl, tc), 0) + base
        goal = jnp.concatenate([targets[b] for b in blks], axis=1)
        hot = (goal == ids).astype(F32).astype(BF16)
        o = jnp.dot(o_t[...], hot, preferred_element_type=F32)
        o_full[c] = o
        for kk in range(2):
            for g in range(nf):
                so[blks[kk] * nf + g] = o[g * rf:(g + 1) * rf, kk * tb:(kk + 1) * tb].astype(BF16)
        for kk in range(2):
            for g in range(nf):
                d = blks[kk] * nf + g
                post(so.at[d], ro.at[me], so_send, ro_sem, d)
        return carry

    lax.fori_loop(0, xn * parts, onehot_step, 0)

    vt = min(256, vl)
    nt = vl // vt

    def tiles(xi, h, lo, hi, m):
        def tile(i, m):
            at = pl.ds(pl.multiple_of(i * vt, vt), vt)
            l = lax.dot_general(head[at, :], hid[xi, h], NT, preferred_element_type=F32)
            lg[at, :] = l
            return jnp.maximum(m, jnp.max(l, axis=0, keepdims=True))
        return lax.fori_loop(lo, hi, tile, m)

    def finish(xi, h, m):
        e = jnp.exp(lg[...] - m)
        s = jnp.sum(e, axis=0, keepdims=True)
        u = jnp.dot(o_t[...], e.astype(BF16), preferred_element_type=F32)
        u = u / s - o_full[xi * parts + h]
        blks = [(2 * xi + kk) * parts + h for kk in range(2)]
        for kk in range(2):
            lanes = slice(kk * tb, (kk + 1) * tb)
            st[blks[kk], 0:1, :] = m[:, lanes]
            st[blks[kk], 1:2, :] = s[:, lanes]
            for g in range(nf):
                sv[blks[kk] * nf + g] = u[g * rf:(g + 1) * rf, lanes].astype(BF16)
        for kk in range(2):
            for g in range(nf):
                d = blks[kk] * nf + g
                post(st.at[blks[kk]], rst.at[me], st_send, rst_sem, d)
                post(sv.at[d], rv.at[me], sv_send, rv_sem, d)
        act = jnp.dot(hid[xi, h], iproj[...], preferred_element_type=F32)
        for kk in range(2):
            ins[blks[kk]] = act[kk * tb:(kk + 1) * tb]

    low = jnp.full((1, tc), -jnp.inf, F32)
    every = range(xn - 1)

    def sibling(h):
        blk = half(x, 1 - k, h)
        remote(blk, blk, own_sems.at[0, h], own_sems.at[1, h], v, sib).wait_recv()

    def arrivals(*which):
        for rel, j in which:
            for r in every:
                arrive(r, rel, j)

    def passed(r, h):
        for rel in range(4):
            for j in range(h * per, (h + 1) * per):
                blk = rows(src_of(r), 1 - k, owners[rel], j)
                remote(blk, blk, s_send.at[r, rel, j], s_recv.at[r, rel, j], v, sib).wait_recv()

    mid = nt // 2
    loads[0].wait()
    loads[1].wait()
    sibling(0)
    arrivals((0, 0))
    m = tiles(x, 0, 0, mid, low)
    arrivals((0, 1))
    m = tiles(x, 0, mid, nt, m)
    arrivals((1, 0), (2, 0), (0, 2))
    finish(x, 0, m)
    sibling(1)
    m = tiles(x, 1, 0, mid, low)
    arrivals((1, 1), (2, 1), (0, 3))
    m = tiles(x, 1, mid, nt, m)
    finish(x, 1, m)
    arrivals((3, 0), (3, 1))
    for r in every:
        passed(r, 0)
        m = tiles(src_of(r), 0, 0, mid, low)
        if r == 0:
            arrivals((1, 2), (2, 2))
        m = tiles(src_of(r), 0, mid, nt, m)
        finish(src_of(r), 0, m)
    arrivals((1, 3), (2, 3), (3, 2), (3, 3))
    for r in every:
        passed(r, 1)
        finish(src_of(r), 1, tiles(src_of(r), 1, 0, nt, low))

    for a, b, i in ((sv, rv, 0), (so, ro, 1)):
        pltpu.make_async_copy(a.at[me], b.at[me], loc_sem.at[i]).start()
    pltpu.make_async_copy(st.at[v], rst.at[me], loc_sem.at[2]).start()
    for a, b, i in ((sv, rv, 0), (so, ro, 1)):
        pltpu.make_async_copy(a.at[me], b.at[me], loc_sem.at[i]).wait()
    pltpu.make_async_copy(st.at[v], rst.at[me], loc_sem.at[2]).wait()

    def take(p, c):
        d = (me + p) % nd
        remote(st.at[v], rst.at[d], st_send.at[d], rst_sem.at[d], v, f).wait_recv()
        remote(so.at[d], ro.at[d], so_send.at[d], ro_sem.at[d], v, f).wait_recv()
        remote(sv.at[d], rv.at[d], sv_send.at[d], rv_sem.at[d], v, f).wait_recv()
        return c

    lax.fori_loop(1, nd, take, 0)
    peak, mass = rst[:, 0, :], rst[:, 1, :]
    mass = jnp.exp(peak - jnp.max(peak, axis=0, keepdims=True)) * mass
    share = mass / jnp.sum(mass, axis=0, keepdims=True)
    acc = jnp.zeros((rf, tb), F32)
    for d in range(nd):
        w = share[d:d + 1, :]
        acc = acc + w * rv[d].astype(F32) - (1.0 - w) * ro[d].astype(F32)
    osb[v] = acc

    def spread(p, c):
        dv = (v + p) % nv
        remote(osb.at[v], osb.at[v], ag_send.at[p], ag_recv.at[v], dv, f).start()
        return c

    lax.fori_loop(1, nv, spread, 0)

    qg[...] = jnp.zeros_like(qg)

    def outer(p, c):
        b = (v + p) % nv

        @pl.when(p > 0)
        def _():
            remote(osb.at[b], osb.at[b], ag_send.at[p], ag_recv.at[b], v, f).wait_recv()

        member = (seqs[b] == lax.broadcasted_iota(jnp.int32, (SEQS, tb), 0)).astype(F32)
        o = osb[b]
        weighted = jnp.concatenate([member * o[i:i + 1, :] for i in range(rf)], axis=0)
        qg[...] += jnp.dot(weighted, ins[b], preferred_element_type=F32, precision=lax.Precision.HIGHEST)
        return c

    lax.fori_loop(0, nv, outer, 0)
    for i in range(rf):
        qgm[:, i * rank:(i + 1) * rank] = qg[i * SEQS:(i + 1) * SEQS, :].astype(BF16)
    loads[2].wait()

    def score(p, c):
        g = (f + p) % nf
        part[g] = lax.dot_general(
            qgm[...], gs[pl.ds(pl.multiple_of(g * eo, eo), eo), :], NT, preferred_element_type=F32)

        @pl.when(p < nf)
        def _():
            remote(part.at[g], infl.at[f], in_send.at[p % nf], in_recv.at[f], v, g).start()
        return c

    lax.fori_loop(1, nf + 1, score, 0)
    result = part[f]
    for p in range(1, nf):
        g = (f + p) % nf
        remote(part.at[g], infl.at[g], in_send.at[p], in_recv.at[g], v, g).wait_recv()
        result = result + infl[g]
    out[...] = result

    for copy in pending:
        copy.wait_send()

    def drain(p, c):
        d = (me + p) % nd
        remote(st.at[d // nf], rst.at[me], st_send.at[d], rst_sem.at[me], v, f).wait_send()
        remote(so.at[d], ro.at[me], so_send.at[d], ro_sem.at[me], v, f).wait_send()
        remote(sv.at[d], rv.at[me], sv_send.at[d], rv_sem.at[me], v, f).wait_send()
        return c

    lax.fori_loop(1, nd, drain, 0)
    for p in range(1, nv):
        remote(osb.at[v], osb.at[v], ag_send.at[p], ag_recv.at[v], v, f).wait_send()
    for p in range(1, nf):
        g = (f + p) % nf
        remote(part.at[g], infl.at[f], in_send.at[p], in_recv.at[f], v, f).wait_send()


def solution(mesh):
    nv, nf = mesh.shape["vocab"], mesh.shape["feat"]
    nd = nv * nf
    xn = nf // 2

    def on_device(hidden, out_head, out_proj, in_proj, targets, seq_ids, grad_store):
        tl, width = hidden.shape
        vl, rank = out_proj.shape
        el, fl = grad_store.shape
        tokens = tl * nf
        rf, tb, eo = rank // nf, tokens // nv, el // nf
        parts = tl // tb
        any_spec = pl.BlockSpec(memory_space=pl.ANY)
        vmem = pl.BlockSpec(memory_space=pltpu.VMEM)
        dma = pltpu.SemaphoreType.DMA
        res = pl.pallas_call(
            functools.partial(kernel, nv, nf),
            out_shape=jax.ShapeDtypeStruct((SEQS, eo), F32),
            in_specs=[any_spec, any_spec, vmem, any_spec, vmem, vmem, any_spec],
            out_specs=vmem,
            scratch_shapes=[
                pltpu.VMEM((xn, parts, 2 * tb, width), BF16),
                pltpu.VMEM((vl, width), BF16),
                pltpu.VMEM((width, rank), BF16),
                pltpu.VMEM((el, fl), BF16),
                pltpu.VMEM((vl, 2 * tb), F32),
                pltpu.VMEM((rank, vl), BF16),
                pltpu.VMEM((xn * parts, rank, 2 * tb), F32),
                pltpu.VMEM((nv, tb, rank), F32),
                pltpu.VMEM((nd, rf, tb), BF16),
                pltpu.VMEM((nd, rf, tb), BF16),
                pltpu.VMEM((nv, 8, tb), F32),
                pltpu.VMEM((nd, rf, tb), BF16),
                pltpu.VMEM((nd, rf, tb), BF16),
                pltpu.VMEM((nd, 8, tb), F32),
                pltpu.VMEM((nv, rf, tb), F32),
                pltpu.VMEM((rf * SEQS, rank), F32),
                pltpu.VMEM((SEQS, fl), BF16),
                pltpu.VMEM((nf, SEQS, eo), F32),
                pltpu.VMEM((nf, SEQS, eo), F32),
                dma((3 + parts,)),
                dma((xn - 1, SUBS)),
                dma((xn - 1, 2, SUBS)),
                dma((xn - 1, 2, SUBS)),
                dma((xn - 1, 4, SUBS)),
                dma((xn - 1, 4, SUBS)),
                dma((xn - 1, 4, SUBS)),
                dma((2, parts)),
                dma((nd,)),
                dma((nd,)),
                dma((nd,)),
                dma((nd,)),
                dma((nd,)),
                dma((nd,)),
                dma((nv,)),
                dma((nv,)),
                dma((nf,)),
                dma((nf,)),
                dma((3,)),
            ],
            compiler_params=pltpu.CompilerParams(
                collective_id=0, has_side_effects=True, vmem_limit_bytes=60 * 1024 * 1024),
        )(hidden, out_head, out_proj, in_proj, targets.reshape(nv, 1, tb), seq_ids.reshape(nv, 1, tb), grad_store)
        return res.T

    in_specs = (
        P("feat", None),
        P(("vocab", "feat"), None),
        P(("vocab", "feat"), None),
        P(),
        P(),
        P(),
        P("vocab", "feat"),
    )
    return jax.shard_map(
        on_device, mesh=mesh, in_specs=in_specs, out_specs=P(("vocab", "feat"), None), check_vma=False
    )
```

```python
import functools

import jax
import jax.numpy as jnp
from jax import lax
from jax.experimental import pallas as pl
from jax.experimental.pallas import tpu as pltpu
from jax.sharding import PartitionSpec as P

SEQS = 16
SUBS = 4
F32 = jnp.float32
BF16 = jnp.bfloat16
NT = (((1,), (1,)), ((), ()))


def kernel(nv, nf, hid_in, head_in, oproj, iproj_in, targets, seqs, gs_in, out,
           hid, head, iproj, gs, lg, o_t, o_full, ins, sv, so, s2, st, rv, r1, ro, rst, osb, qg, qgm, part, infl,
           load_sem, x_send, y_send, z_send, s_send, recv, s_recv, own_sems,
           sv_send, so_send, s2_send, st_send, rv_sem, r1_sem, ro_sem, rst_sem, ag_send, ag_recv, in_send, in_recv, loc_sem, heard):
    v = lax.axis_index("vocab")
    f = lax.axis_index("feat")
    me = v * nf + f
    nd = nv * nf
    x, k = f // 2, f % 2
    xn = nf // 2
    sib = f + 1 - 2 * k
    vy = v + 1 - 2 * (v % 2)
    vz = v + 2 - 4 * ((v // 2) % 2)
    vl = head.shape[0]
    rank = oproj.shape[1]
    rf, tb = sv.shape[1], sv.shape[2]
    parts = hid.shape[1]
    tc = 2 * tb
    eo = out.shape[1]
    piece = tb // 4
    per = SUBS // parts
    sr = piece // per

    loads = [
        pltpu.make_async_copy(head_in, head, load_sem.at[0]),
        pltpu.make_async_copy(iproj_in, iproj, load_sem.at[1]),
        pltpu.make_async_copy(gs_in, gs, load_sem.at[2]),
    ]

    def half(xi, kk, h):
        return hid.at[xi, h, pl.ds(pl.multiple_of(kk * tb, tb), tb)]

    mine = [pltpu.make_async_copy(hid_in.at[pl.ds(h * tb, tb)], half(x, k, h), load_sem.at[3 + h])
            for h in range(parts)]
    for copy in mine + loads[:2]:
        copy.start()

    def flip(i, bit):
        return i + bit - 2 * bit * ((i // bit) % 2)

    near = [(v, flip(f, 1 << i)) for i in range(nf.bit_length() - 1)]
    near += [(flip(v, 1 << i), f) for i in range(nv.bit_length() - 1)]
    barrier = pltpu.get_barrier_semaphore()

    def signal(sem, place):
        pl.semaphore_signal(sem, inc=1, device_id={"vocab": place[0], "feat": place[1]},
                            device_id_type=pl.DeviceIdType.MESH)

    for place in near:
        signal(barrier, place)
    pl.semaphore_wait(barrier, len(near))

    def hear(lo, hi):
        for i in range(lo, hi):
            signal(heard.at[i], near[i])
            pl.semaphore_wait(heard.at[i], 1)

    hear(0, nf.bit_length() - 1)

    def remote(src, dst, ss, rs, dv, df):
        return pltpu.make_async_remote_copy(
            src_ref=src, dst_ref=dst, send_sem=ss, recv_sem=rs,
            device_id={"vocab": dv, "feat": df}, device_id_type=pl.DeviceIdType.MESH)

    def rows(xi, kk, owner, j):
        at = kk * tb + (owner % 4) * piece + (j % per) * sr
        return hid.at[xi, j // per, pl.ds(pl.multiple_of(at, sr), sr)]

    pending = []

    def go(copy):
        copy.start()
        pending.append(copy)

    for h in range(parts):
        mine[h].wait()
        for r in range(xn - 1):
            fo = 2 * ((x + r + 1) % xn) + k
            for j in range(h * per, (h + 1) * per):
                blk = rows(x, k, v, j)
                go(remote(blk, blk, x_send.at[r, j], recv.at[r, 0, j], v, fo))
        go(remote(half(x, k, h), half(x, k, h), own_sems.at[0, h], own_sems.at[1, h], v, sib))
    loads[2].start()

    def src_of(r):
        return (x + xn - r - 1) % xn

    vd = vy + vz - v
    owners = (v, vy, vz, vd)

    def arrive(r, rel, j):
        blk = rows(src_of(r), k, owners[rel], j)
        remote(blk, blk, x_send.at[r, j], recv.at[r, rel, j], v, f).wait_recv()
        first = j % per < per // 2
        if rel == 0:
            go(remote(blk, blk, y_send.at[r, 0, j], recv.at[r, 1, j], vy, f))
            go(remote(blk, blk, z_send.at[r, 0, j], recv.at[r, 2, j], vz, f))
        if rel == 1 and first:
            go(remote(blk, blk, z_send.at[r, 1, j], recv.at[r, 3, j], vz, f))
        if rel == 2 and not first:
            go(remote(blk, blk, y_send.at[r, 1, j], recv.at[r, 3, j], vy, f))
        go(remote(blk, blk, s_send.at[r, rel, j], s_recv.at[r, rel, j], v, sib))

    def post(send_buf, recv_buf, sends, recvs, d):
        @pl.when(d != me)
        def _():
            remote(send_buf, recv_buf, sends.at[d], recvs.at[me], d // nf, d % nf).start()

    o_t[...] = oproj[...].astype(F32).T.astype(BF16)
    base = me * vl

    def onehot_step(c, carry):
        xi, h = c // parts, c % parts
        blks = [(2 * xi + kk) * parts + h for kk in range(2)]
        ids = lax.broadcasted_iota(jnp.int32, (vl, tc), 0) + base
        goal = jnp.concatenate([targets[b] for b in blks], axis=1)
        hot = (goal == ids).astype(F32).astype(BF16)
        o = jnp.dot(o_t[...], hot, preferred_element_type=F32)
        o_full[c] = o
        for kk in range(2):
            for g in range(nf):
                so[g, blks[kk]] = o[g * rf:(g + 1) * rf, kk * tb:(kk + 1) * tb].astype(BF16)
        return carry

    lax.fori_loop(0, xn * parts, onehot_step, 0)
    hear(nf.bit_length() - 1, len(near))
    for p in range(1, nf):
        g = (f + p) % nf
        go(remote(so.at[g], r1.at[f], so_send.at[p], r1_sem.at[f], v, g))

    def onehot_sum():
        for p in range(1, nf):
            g = (f + p) % nf
            remote(so.at[g], r1.at[g], so_send.at[p], r1_sem.at[g], v, g).wait_recv()

        def one(b, c):
            t = so[f, b].astype(F32)
            for p in range(1, nf):
                t = t + r1[(f + p) % nf, b].astype(F32)
            s2[b] = t.astype(BF16)
            return c

        lax.fori_loop(0, nv, one, 0)
        for p in range(1, nv):
            b = (v + p) % nv
            go(remote(s2.at[b], ro.at[v], s2_send.at[p], ro_sem.at[v], b, f))

    vt = min(256, vl)
    nt = vl // vt

    def tiles(xi, h, lo, hi, m):
        def tile(i, m):
            at = pl.ds(pl.multiple_of(i * vt, vt), vt)
            l = lax.dot_general(head[at, :], hid[xi, h], NT, preferred_element_type=F32)
            lg[at, :] = l
            return jnp.maximum(m, jnp.max(l, axis=0, keepdims=True))
        return lax.fori_loop(lo, hi, tile, m)

    def finish(xi, h, m):
        e = jnp.exp(lg[...] - m)
        s = jnp.sum(e, axis=0, keepdims=True)
        u = jnp.dot(o_t[...], e.astype(BF16), preferred_element_type=F32)
        u = u / s - o_full[xi * parts + h]
        blks = [(2 * xi + kk) * parts + h for kk in range(2)]
        for kk in range(2):
            lanes = slice(kk * tb, (kk + 1) * tb)
            st[blks[kk], 0:1, :] = m[:, lanes]
            st[blks[kk], 1:2, :] = s[:, lanes]
            for g in range(nf):
                sv[blks[kk] * nf + g] = u[g * rf:(g + 1) * rf, lanes].astype(BF16)
        for kk in range(2):
            for g in range(nf):
                d = blks[kk] * nf + g
                post(st.at[blks[kk]], rst.at[me], st_send, rst_sem, d)
                post(sv.at[d], rv.at[me], sv_send, rv_sem, d)
        act = jnp.dot(hid[xi, h], iproj[...], preferred_element_type=F32)
        for kk in range(2):
            ins[blks[kk]] = act[kk * tb:(kk + 1) * tb]

    low = jnp.full((1, tc), -jnp.inf, F32)
    every = range(xn - 1)

    def sibling(h):
        blk = half(x, 1 - k, h)
        remote(blk, blk, own_sems.at[0, h], own_sems.at[1, h], v, sib).wait_recv()

    def arrivals(*which):
        for rel, j in which:
            for r in every:
                arrive(r, rel, j)

    def passed(r, h):
        for rel in range(4):
            for j in range(h * per, (h + 1) * per):
                blk = rows(src_of(r), 1 - k, owners[rel], j)
                remote(blk, blk, s_send.at[r, rel, j], s_recv.at[r, rel, j], v, sib).wait_recv()

    mid = nt // 2
    loads[0].wait()
    loads[1].wait()
    sibling(0)
    arrivals((0, 0))
    m = tiles(x, 0, 0, mid, low)
    arrivals((0, 1))
    m = tiles(x, 0, mid, nt, m)
    arrivals((1, 0), (2, 0), (0, 2))
    finish(x, 0, m)
    sibling(1)
    m = tiles(x, 1, 0, mid, low)
    arrivals((1, 1), (2, 1), (0, 3))
    m = tiles(x, 1, mid, nt, m)
    finish(x, 1, m)
    onehot_sum()
    arrivals((3, 0), (3, 1))
    for r in every:
        passed(r, 0)
        m = tiles(src_of(r), 0, 0, mid, low)
        if r == 0:
            arrivals((1, 2), (2, 2))
        m = tiles(src_of(r), 0, mid, nt, m)
        finish(src_of(r), 0, m)
    arrivals((1, 3), (2, 3), (3, 2), (3, 3))
    for r in every:
        passed(r, 1)
        finish(src_of(r), 1, tiles(src_of(r), 1, 0, nt, low))

    local = [pltpu.make_async_copy(sv.at[me], rv.at[me], loc_sem.at[0]),
             pltpu.make_async_copy(st.at[v], rst.at[me], loc_sem.at[1])]
    for copy in local:
        copy.start()
    targeted = s2[v].astype(F32)
    for p in range(1, nv):
        b = (v + p) % nv
        remote(s2.at[b], ro.at[b], s2_send.at[p], ro_sem.at[b], v, f).wait_recv()
        targeted = targeted + ro[b].astype(F32)
    for copy in local:
        copy.wait()

    def take(p, c):
        d = (me + p) % nd
        remote(st.at[v], rst.at[d], st_send.at[d], rst_sem.at[d], v, f).wait_recv()
        remote(sv.at[d], rv.at[d], sv_send.at[d], rv_sem.at[d], v, f).wait_recv()
        return c

    lax.fori_loop(1, nd, take, 0)
    peak, mass = rst[:, 0, :], rst[:, 1, :]
    mass = jnp.exp(peak - jnp.max(peak, axis=0, keepdims=True)) * mass
    share = mass / jnp.sum(mass, axis=0, keepdims=True)
    first_row = lax.broadcasted_iota(jnp.int32, (nd, tb), 0) * vl
    goal = targets[v]
    outside = (goal < first_row) | (goal >= first_row + vl)
    acc = -jnp.sum(jnp.where(outside, share, 0.0), axis=0, keepdims=True) * targeted
    for d in range(nd):
        w = share[d:d + 1, :]
        acc = acc + w * rv[d].astype(F32)
    osb[v] = acc

    def spread(p, c):
        dv = (v + p) % nv
        remote(osb.at[v], osb.at[v], ag_send.at[p], ag_recv.at[v], dv, f).start()
        return c

    lax.fori_loop(1, nv, spread, 0)

    qg[...] = jnp.zeros_like(qg)

    def outer(p, c):
        b = (v + p) % nv

        @pl.when(p > 0)
        def _():
            remote(osb.at[b], osb.at[b], ag_send.at[p], ag_recv.at[b], v, f).wait_recv()

        member = (seqs[b] == lax.broadcasted_iota(jnp.int32, (SEQS, tb), 0)).astype(F32)
        o = osb[b]
        weighted = jnp.concatenate([member * o[i:i + 1, :] for i in range(rf)], axis=0)
        qg[...] += jnp.dot(weighted, ins[b], preferred_element_type=F32, precision=lax.Precision.HIGHEST)
        return c

    lax.fori_loop(0, nv, outer, 0)
    for i in range(rf):
        qgm[:, i * rank:(i + 1) * rank] = qg[i * SEQS:(i + 1) * SEQS, :].astype(BF16)
    loads[2].wait()

    def score(p, c):
        g = (f + p) % nf
        part[g] = lax.dot_general(
            qgm[...], gs[pl.ds(pl.multiple_of(g * eo, eo), eo), :], NT, preferred_element_type=F32)

        @pl.when(p < nf)
        def _():
            remote(part.at[g], infl.at[f], in_send.at[p % nf], in_recv.at[f], v, g).start()
        return c

    lax.fori_loop(1, nf + 1, score, 0)
    result = part[f]
    for p in range(1, nf):
        g = (f + p) % nf
        remote(part.at[g], infl.at[g], in_send.at[p], in_recv.at[g], v, g).wait_recv()
        result = result + infl[g]
    out[...] = result

    for copy in pending:
        copy.wait_send()

    def drain(p, c):
        d = (me + p) % nd
        remote(st.at[d // nf], rst.at[me], st_send.at[d], rst_sem.at[me], v, f).wait_send()
        remote(sv.at[d], rv.at[me], sv_send.at[d], rv_sem.at[me], v, f).wait_send()
        return c

    lax.fori_loop(1, nd, drain, 0)
    for p in range(1, nv):
        remote(osb.at[v], osb.at[v], ag_send.at[p], ag_recv.at[v], v, f).wait_send()
    for p in range(1, nf):
        g = (f + p) % nf
        remote(part.at[g], infl.at[f], in_send.at[p], in_recv.at[f], v, f).wait_send()


def solution(mesh):
    nv, nf = mesh.shape["vocab"], mesh.shape["feat"]
    nd = nv * nf
    xn = nf // 2

    def on_device(hidden, out_head, out_proj, in_proj, targets, seq_ids, grad_store):
        tl, width = hidden.shape
        vl, rank = out_proj.shape
        el, fl = grad_store.shape
        tokens = tl * nf
        rf, tb, eo = rank // nf, tokens // nv, el // nf
        parts = tl // tb
        any_spec = pl.BlockSpec(memory_space=pl.ANY)
        vmem = pl.BlockSpec(memory_space=pltpu.VMEM)
        dma = pltpu.SemaphoreType.DMA
        res = pl.pallas_call(
            functools.partial(kernel, nv, nf),
            out_shape=jax.ShapeDtypeStruct((SEQS, eo), F32),
            in_specs=[any_spec, any_spec, vmem, any_spec, vmem, vmem, any_spec],
            out_specs=vmem,
            scratch_shapes=[
                pltpu.VMEM((xn, parts, 2 * tb, width), BF16),
                pltpu.VMEM((vl, width), BF16),
                pltpu.VMEM((width, rank), BF16),
                pltpu.VMEM((el, fl), BF16),
                pltpu.VMEM((vl, 2 * tb), F32),
                pltpu.VMEM((rank, vl), BF16),
                pltpu.VMEM((xn * parts, rank, 2 * tb), F32),
                pltpu.VMEM((nv, tb, rank), F32),
                pltpu.VMEM((nd, rf, tb), BF16),
                pltpu.VMEM((nf, nv, rf, tb), BF16),
                pltpu.VMEM((nv, rf, tb), BF16),
                pltpu.VMEM((nv, 2, tb), F32),
                pltpu.VMEM((nd, rf, tb), BF16),
                pltpu.VMEM((nf, nv, rf, tb), BF16),
                pltpu.VMEM((nv, rf, tb), BF16),
                pltpu.VMEM((nd, 2, tb), F32),
                pltpu.VMEM((nv, rf, tb), F32),
                pltpu.VMEM((rf * SEQS, rank), F32),
                pltpu.VMEM((SEQS, fl), BF16),
                pltpu.VMEM((nf, SEQS, eo), F32),
                pltpu.VMEM((nf, SEQS, eo), F32),
                dma((3 + parts,)),
                dma((xn - 1, SUBS)),
                dma((xn - 1, 2, SUBS)),
                dma((xn - 1, 2, SUBS)),
                dma((xn - 1, 4, SUBS)),
                dma((xn - 1, 4, SUBS)),
                dma((xn - 1, 4, SUBS)),
                dma((2, parts)),
                dma((nd,)),
                dma((nf,)),
                dma((nv,)),
                dma((nd,)),
                dma((nd,)),
                dma((nf,)),
                dma((nv,)),
                dma((nd,)),
                dma((nv,)),
                dma((nv,)),
                dma((nf,)),
                dma((nf,)),
                dma((2,)),
                pltpu.SemaphoreType.REGULAR((nf.bit_length() + nv.bit_length() - 2,)),
            ],
            compiler_params=pltpu.CompilerParams(
                collective_id=0, has_side_effects=True, vmem_limit_bytes=60 * 1024 * 1024),
        )(hidden, out_head, out_proj, in_proj, targets.reshape(nv, 1, tb), seq_ids.reshape(nv, 1, tb), grad_store)
        return res.T

    in_specs = (
        P("feat", None),
        P(("vocab", "feat"), None),
        P(("vocab", "feat"), None),
        P(),
        P(),
        P(),
        P("vocab", "feat"),
    )
    return jax.shard_map(
        on_device, mesh=mesh, in_specs=in_specs, out_specs=P(("vocab", "feat"), None), check_vma=False
    )
```

```python
import functools

import jax
import jax.numpy as jnp
from jax import lax
from jax.experimental import pallas as pl
from jax.experimental.pallas import tpu as pltpu
from jax.sharding import PartitionSpec as P

SEQS = 16
SUBS = 4
F32 = jnp.float32
BF16 = jnp.bfloat16
NT = (((1,), (1,)), ((), ()))


def kernel(nv, nf, hid_in, head_in, oproj, iproj_in, targets, seqs, gs_in, out,
           hid, head, iproj, gs, lg, o_t, o_full, ins, sv, so, s2, st, rv, r1, ro, rst, osb, qg, qgm, part, infl,
           load_sem, x_send, y_send, z_send, s_send, recv, s_recv, own_sems,
           sv_send, so_send, s2_send, st_send, rv_sem, r1_sem, ro_sem, rst_sem, ag_send, ag_recv, in_send, in_recv, loc_sem, heard):
    v = lax.axis_index("vocab")
    f = lax.axis_index("feat")
    me = v * nf + f
    nd = nv * nf
    x, k = f // 2, f % 2
    xn = nf // 2
    sib = f + 1 - 2 * k
    vy = v + 1 - 2 * (v % 2)
    vz = v + 2 - 4 * ((v // 2) % 2)
    vd = vy + vz - v
    vl = head.shape[0]
    rank = oproj.shape[1]
    rf, tb = sv.shape[1], sv.shape[2]
    parts = hid.shape[1]
    tc = 2 * tb
    eo = out.shape[1]
    piece = tb // 4
    per = SUBS // parts
    sr = piece // per

    loads = [
        pltpu.make_async_copy(head_in, head, load_sem.at[0]),
        pltpu.make_async_copy(iproj_in, iproj, load_sem.at[1]),
        pltpu.make_async_copy(gs_in, gs, load_sem.at[2]),
    ]

    def half(xi, kk, h):
        return hid.at[xi, h, pl.ds(pl.multiple_of(kk * tb, tb), tb)]

    mine = [pltpu.make_async_copy(hid_in.at[pl.ds(h * tb, tb)], half(x, k, h), load_sem.at[3 + h])
            for h in range(parts)]
    for copy in mine + loads[:2]:
        copy.start()

    def flip(i, bit):
        return i + bit - 2 * bit * ((i // bit) % 2)

    near = [(v, flip(f, 1 << i)) for i in range(nf.bit_length() - 1)]
    near += [(flip(v, 1 << i), f) for i in range(nv.bit_length() - 1)]
    barrier = pltpu.get_barrier_semaphore()

    def signal(sem, place):
        pl.semaphore_signal(sem, inc=1, device_id={"vocab": place[0], "feat": place[1]},
                            device_id_type=pl.DeviceIdType.MESH)

    for place in near:
        signal(barrier, place)
    pl.semaphore_wait(barrier, len(near))

    def hear(lo, hi):
        for i in range(lo, hi):
            signal(heard.at[i], near[i])
            pl.semaphore_wait(heard.at[i], 1)

    hear(0, nf.bit_length() - 1)

    def remote(src, dst, ss, rs, dv, df):
        return pltpu.make_async_remote_copy(
            src_ref=src, dst_ref=dst, send_sem=ss, recv_sem=rs,
            device_id={"vocab": dv, "feat": df}, device_id_type=pl.DeviceIdType.MESH)

    def rows(xi, kk, owner, j):
        at = kk * tb + (owner % 4) * piece + (j % per) * sr
        return hid.at[xi, j // per, pl.ds(pl.multiple_of(at, sr), sr)]

    pending = []

    def go(copy):
        copy.start()
        pending.append(copy)

    for h in range(parts):
        mine[h].wait()
        for r in range(xn - 1):
            fo = 2 * ((x + r + 1) % xn) + k
            for j in range(h * per, (h + 1) * per):
                blk = rows(x, k, v, j)
                go(remote(blk, blk, x_send.at[r, j], recv.at[r, 0, j], v, fo))
        if h == parts - 1:
            for r in range(xn - 1):
                fo = 2 * ((x + r + 1) % xn) + k
                for j in range(h * per, (h + 1) * per):
                    blk = rows(x, k, vd, j)
                    go(remote(blk, blk, x_send.at[r, j + per], recv.at[r, 3, j], v, fo))
        go(remote(half(x, k, h), half(x, k, h), own_sems.at[0, h], own_sems.at[1, h], v, sib))
    loads[2].start()

    def src_of(r):
        return (x + xn - r - 1) % xn

    owners = (v, vy, vz, vd)

    def arrive(r, rel, j):
        blk = rows(src_of(r), k, owners[rel], j)
        remote(blk, blk, x_send.at[r, j], recv.at[r, rel, j], v, f).wait_recv()
        first = j % per < per // 2
        relay = j // per < parts - 1
        if rel == 0:
            go(remote(blk, blk, y_send.at[r, 0, j], recv.at[r, 1, j], vy, f))
            go(remote(blk, blk, z_send.at[r, 0, j], recv.at[r, 2, j], vz, f))
        if rel == 1 and relay and first:
            go(remote(blk, blk, z_send.at[r, 1, j], recv.at[r, 3, j], vz, f))
        if rel == 2 and relay and not first:
            go(remote(blk, blk, y_send.at[r, 1, j], recv.at[r, 3, j], vy, f))
        go(remote(blk, blk, s_send.at[r, rel, j], s_recv.at[r, rel, j], v, sib))

    def post(send_buf, recv_buf, sends, recvs, d):
        @pl.when(d != me)
        def _():
            remote(send_buf, recv_buf, sends.at[d], recvs.at[me], d // nf, d % nf).start()

    o_t[...] = oproj[...].astype(F32).T.astype(BF16)
    base = me * vl

    def onehot_step(c, carry):
        xi, h = c // parts, c % parts
        blks = [(2 * xi + kk) * parts + h for kk in range(2)]
        ids = lax.broadcasted_iota(jnp.int32, (vl, tc), 0) + base
        goal = jnp.concatenate([targets[b] for b in blks], axis=1)
        hot = (goal == ids).astype(F32).astype(BF16)
        o = jnp.dot(o_t[...], hot, preferred_element_type=F32)
        o_full[c] = o
        for kk in range(2):
            for g in range(nf):
                so[g, blks[kk]] = o[g * rf:(g + 1) * rf, kk * tb:(kk + 1) * tb].astype(BF16)
        return carry

    lax.fori_loop(0, xn * parts, onehot_step, 0)
    hear(nf.bit_length() - 1, len(near))
    for p in range(1, nf):
        g = (f + p) % nf
        go(remote(so.at[g], r1.at[f], so_send.at[p], r1_sem.at[f], v, g))

    def onehot_sum():
        for p in range(1, nf):
            g = (f + p) % nf
            remote(so.at[g], r1.at[g], so_send.at[p], r1_sem.at[g], v, g).wait_recv()

        def one(b, c):
            t = so[f, b].astype(F32)
            for p in range(1, nf):
                t = t + r1[(f + p) % nf, b].astype(F32)
            s2[b] = t.astype(BF16)
            return c

        lax.fori_loop(0, nv, one, 0)
        for p in range(1, nv):
            b = (v + p) % nv
            go(remote(s2.at[b], ro.at[v], s2_send.at[p], ro_sem.at[v], b, f))

    vt = min(256, vl)
    nt = vl // vt

    def tiles(xi, h, lo, hi, m):
        def tile(i, m):
            at = pl.ds(pl.multiple_of(i * vt, vt), vt)
            l = lax.dot_general(head[at, :], hid[xi, h], NT, preferred_element_type=F32)
            lg[at, :] = l
            return jnp.maximum(m, jnp.max(l, axis=0, keepdims=True))
        return lax.fori_loop(lo, hi, tile, m)

    def finish(xi, h, m):
        e = jnp.exp(lg[...] - m)
        s = jnp.sum(e, axis=0, keepdims=True)
        u = jnp.dot(o_t[...], e.astype(BF16), preferred_element_type=F32)
        u = u / s - o_full[xi * parts + h]
        blks = [(2 * xi + kk) * parts + h for kk in range(2)]
        for kk in range(2):
            lanes = slice(kk * tb, (kk + 1) * tb)
            st[blks[kk], 0:1, :] = m[:, lanes]
            st[blks[kk], 1:2, :] = s[:, lanes]
            for g in range(nf):
                sv[blks[kk] * nf + g] = u[g * rf:(g + 1) * rf, lanes].astype(BF16)
        for kk in range(2):
            for g in range(nf):
                d = blks[kk] * nf + g
                post(st.at[blks[kk]], rst.at[me], st_send, rst_sem, d)
                post(sv.at[d], rv.at[me], sv_send, rv_sem, d)
        act = jnp.dot(hid[xi, h], iproj[...], preferred_element_type=F32)
        for kk in range(2):
            ins[blks[kk]] = act[kk * tb:(kk + 1) * tb]

    low = jnp.full((1, tc), -jnp.inf, F32)
    every = range(xn - 1)

    def sibling(h):
        blk = half(x, 1 - k, h)
        remote(blk, blk, own_sems.at[0, h], own_sems.at[1, h], v, sib).wait_recv()

    def arrivals(*which):
        for rel, j in which:
            for r in every:
                arrive(r, rel, j)

    def passed(r, h):
        for rel in range(4):
            for j in range(h * per, (h + 1) * per):
                blk = rows(src_of(r), 1 - k, owners[rel], j)
                remote(blk, blk, s_send.at[r, rel, j], s_recv.at[r, rel, j], v, sib).wait_recv()

    mid = nt // 2
    loads[0].wait()
    loads[1].wait()
    sibling(0)
    arrivals((0, 0))
    m = tiles(x, 0, 0, mid, low)
    arrivals((0, 1))
    m = tiles(x, 0, mid, nt, m)
    arrivals((1, 0), (2, 0), (0, 2))
    finish(x, 0, m)
    sibling(1)
    m = tiles(x, 1, 0, mid, low)
    arrivals((1, 1), (2, 1), (0, 3))
    m = tiles(x, 1, mid, nt, m)
    finish(x, 1, m)
    onehot_sum()
    arrivals((3, 0), (3, 1))
    for r in every:
        passed(r, 0)
        m = tiles(src_of(r), 0, 0, mid, low)
        if r == 0:
            arrivals((1, 2), (2, 2))
        m = tiles(src_of(r), 0, mid, nt, m)
        finish(src_of(r), 0, m)
    arrivals((3, 2), (3, 3), (1, 3), (2, 3))
    for r in every:
        passed(r, 1)
        finish(src_of(r), 1, tiles(src_of(r), 1, 0, nt, low))

    local = [pltpu.make_async_copy(sv.at[me], rv.at[me], loc_sem.at[0]),
             pltpu.make_async_copy(st.at[v], rst.at[me], loc_sem.at[1])]
    for copy in local:
        copy.start()
    targeted = s2[v].astype(F32)
    for p in range(1, nv):
        b = (v + p) % nv
        remote(s2.at[b], ro.at[b], s2_send.at[p], ro_sem.at[b], v, f).wait_recv()
        targeted = targeted + ro[b].astype(F32)
    for copy in local:
        copy.wait()

    def take(p, c):
        d = (me + p) % nd
        remote(st.at[v], rst.at[d], st_send.at[d], rst_sem.at[d], v, f).wait_recv()
        remote(sv.at[d], rv.at[d], sv_send.at[d], rv_sem.at[d], v, f).wait_recv()
        return c

    lax.fori_loop(1, nd, take, 0)
    peak, mass = rst[:, 0, :], rst[:, 1, :]
    mass = jnp.exp(peak - jnp.max(peak, axis=0, keepdims=True)) * mass
    share = mass / jnp.sum(mass, axis=0, keepdims=True)
    first_row = lax.broadcasted_iota(jnp.int32, (nd, tb), 0) * vl
    goal = targets[v]
    outside = (goal < first_row) | (goal >= first_row + vl)
    acc = -jnp.sum(jnp.where(outside, share, 0.0), axis=0, keepdims=True) * targeted
    for d in range(nd):
        w = share[d:d + 1, :]
        acc = acc + w * rv[d].astype(F32)
    osb[v] = acc

    def spread(p, c):
        dv = (v + p) % nv
        remote(osb.at[v], osb.at[v], ag_send.at[p], ag_recv.at[v], dv, f).start()
        return c

    lax.fori_loop(1, nv, spread, 0)

    qg[...] = jnp.zeros_like(qg)

    def outer(p, c):
        b = (v + p) % nv

        @pl.when(p > 0)
        def _():
            remote(osb.at[b], osb.at[b], ag_send.at[p], ag_recv.at[b], v, f).wait_recv()

        member = (seqs[b] == lax.broadcasted_iota(jnp.int32, (SEQS, tb), 0)).astype(F32)
        o = osb[b]
        weighted = jnp.concatenate([member * o[i:i + 1, :] for i in range(rf)], axis=0)
        qg[...] += jnp.dot(weighted, ins[b], preferred_element_type=F32, precision=lax.Precision.HIGHEST)
        return c

    lax.fori_loop(0, nv, outer, 0)
    for i in range(rf):
        qgm[:, i * rank:(i + 1) * rank] = qg[i * SEQS:(i + 1) * SEQS, :].astype(BF16)
    loads[2].wait()

    def score(p, c):
        t = p + 1
        g = 2 * ((x + t // 2) % xn) + (k + 1 + t % 2) % 2
        part[g] = lax.dot_general(
            qgm[...], gs[pl.ds(pl.multiple_of(g * eo, eo), eo), :], NT, preferred_element_type=F32)

        @pl.when(p < nf)
        def _():
            remote(part.at[g], infl.at[f], in_send.at[p % nf], in_recv.at[f], v, g).start()
        return c

    lax.fori_loop(1, nf + 1, score, 0)
    result = part[f]
    for p in range(1, nf):
        g = (f + p) % nf
        remote(part.at[g], infl.at[g], in_send.at[p], in_recv.at[g], v, g).wait_recv()
        result = result + infl[g]
    out[...] = result

    for copy in pending:
        copy.wait_send()

    def drain(p, c):
        d = (me + p) % nd
        remote(st.at[d // nf], rst.at[me], st_send.at[d], rst_sem.at[me], v, f).wait_send()
        remote(sv.at[d], rv.at[me], sv_send.at[d], rv_sem.at[me], v, f).wait_send()
        return c

    lax.fori_loop(1, nd, drain, 0)
    for p in range(1, nv):
        remote(osb.at[v], osb.at[v], ag_send.at[p], ag_recv.at[v], v, f).wait_send()
    for p in range(1, nf):
        g = (f + p) % nf
        remote(part.at[g], infl.at[f], in_send.at[p], in_recv.at[f], v, f).wait_send()


def solution(mesh):
    nv, nf = mesh.shape["vocab"], mesh.shape["feat"]
    nd = nv * nf
    xn = nf // 2

    def on_device(hidden, out_head, out_proj, in_proj, targets, seq_ids, grad_store):
        tl, width = hidden.shape
        vl, rank = out_proj.shape
        el, fl = grad_store.shape
        tokens = tl * nf
        rf, tb, eo = rank // nf, tokens // nv, el // nf
        parts = tl // tb
        any_spec = pl.BlockSpec(memory_space=pl.ANY)
        vmem = pl.BlockSpec(memory_space=pltpu.VMEM)
        dma = pltpu.SemaphoreType.DMA
        res = pl.pallas_call(
            functools.partial(kernel, nv, nf),
            out_shape=jax.ShapeDtypeStruct((SEQS, eo), F32),
            in_specs=[any_spec, any_spec, vmem, any_spec, vmem, vmem, any_spec],
            out_specs=vmem,
            scratch_shapes=[
                pltpu.VMEM((xn, parts, 2 * tb, width), BF16),
                pltpu.VMEM((vl, width), BF16),
                pltpu.VMEM((width, rank), BF16),
                pltpu.VMEM((el, fl), BF16),
                pltpu.VMEM((vl, 2 * tb), F32),
                pltpu.VMEM((rank, vl), BF16),
                pltpu.VMEM((xn * parts, rank, 2 * tb), F32),
                pltpu.VMEM((nv, tb, rank), F32),
                pltpu.VMEM((nd, rf, tb), BF16),
                pltpu.VMEM((nf, nv, rf, tb), BF16),
                pltpu.VMEM((nv, rf, tb), BF16),
                pltpu.VMEM((nv, 2, tb), F32),
                pltpu.VMEM((nd, rf, tb), BF16),
                pltpu.VMEM((nf, nv, rf, tb), BF16),
                pltpu.VMEM((nv, rf, tb), BF16),
                pltpu.VMEM((nd, 2, tb), F32),
                pltpu.VMEM((nv, rf, tb), F32),
                pltpu.VMEM((rf * SEQS, rank), F32),
                pltpu.VMEM((SEQS, fl), BF16),
                pltpu.VMEM((nf, SEQS, eo), F32),
                pltpu.VMEM((nf, SEQS, eo), F32),
                dma((3 + parts,)),
                dma((xn - 1, SUBS + SUBS // parts)),
                dma((xn - 1, 2, SUBS)),
                dma((xn - 1, 2, SUBS)),
                dma((xn - 1, 4, SUBS)),
                dma((xn - 1, 4, SUBS)),
                dma((xn - 1, 4, SUBS)),
                dma((2, parts)),
                dma((nd,)),
                dma((nf,)),
                dma((nv,)),
                dma((nd,)),
                dma((nd,)),
                dma((nf,)),
                dma((nv,)),
                dma((nd,)),
                dma((nv,)),
                dma((nv,)),
                dma((nf,)),
                dma((nf,)),
                dma((2,)),
                pltpu.SemaphoreType.REGULAR((nf.bit_length() + nv.bit_length() - 2,)),
            ],
            compiler_params=pltpu.CompilerParams(
                collective_id=0, has_side_effects=True, vmem_limit_bytes=60 * 1024 * 1024),
        )(hidden, out_head, out_proj, in_proj, targets.reshape(nv, 1, tb), seq_ids.reshape(nv, 1, tb), grad_store)
        return res.T

    in_specs = (
        P("feat", None),
        P(("vocab", "feat"), None),
        P(("vocab", "feat"), None),
        P(),
        P(),
        P(),
        P("vocab", "feat"),
    )
    return jax.shard_map(
        on_device, mesh=mesh, in_specs=in_specs, out_specs=P(("vocab", "feat"), None), check_vma=False
    )
```
